32 devices in a mesh: cell: 16 (over z, x, core), rcv: 2 (over y).
Axes of the slice: x: 2, y: 2, z: 4, core: 2. Of those that a mesh axis runs over, the one named last changes fastest.
Arguments:
- green: float32 [1024, 32768], P('rcv', 'cell'), may hold values from -0.03125 to 0.03125
- field: float32 [32768, 512], P('cell'), may hold values from -6 to 6
- probe: float32 [4, 32768], P(None, 'cell'), may hold values from -6 to 6
- cov_inv: float32 [1024, 1024], P('rcv'), as said below
Outputs:
- hessian: float32 [4, 32768], P(None, 'cell')
- curvature: float32 [4, 4], replicated
The draws below stay inside these ranges and needn't reach their ends.
Inputs may be any that keep to these rules, and one draw needn't show every extreme that they name: `cov_inv`: symmetric positive definite.
All inputs are finite; a program needn't handle non-finite values.
Results may differ from the reference program's by a relative error of at most 0.0001.
Values sent between devices are 32-bit elements; how exact they have to be, the bound alone decides.
No kernel may reach another device: no remote copies, remote signals or barrier semaphores. Data moves between devices by JAX's collectives and lax.ppermute only.
A program may use at most 128 MiB of HBM per device.

```python
import jax
import jax.numpy as jnp
from jax import lax

RECEIVER_COUNT = 1024
SOURCE_COUNT = 512
PROBE_COUNT = 4
CELL_DEV = 2048
CELLS = 32768


def draw_cov_inv(key, part):
    base = jax.random.fold_in(key, 11)
    key_mix, key_diag = jax.random.split(base)
    mixing_matrix = jax.random.normal(key_mix, (RECEIVER_COUNT, RECEIVER_COUNT), jnp.float32) * (0.5 / RECEIVER_COUNT ** 0.5)
    levels = jnp.exp(jax.random.uniform(key_diag, (RECEIVER_COUNT,), jnp.float32) * jnp.log(2.0))
    matrix = jnp.dot(mixing_matrix, mixing_matrix.T, precision=lax.Precision.HIGHEST) + jnp.diag(levels)
    return matrix


def block_levels(own_key, shape, cuts, low, top_value):
    gain = 1.0
    for axis_at, parts in cuts:
        heights = jax.random.uniform(jax.random.fold_in(jax.random.fold_in(own_key, 6), axis_at), (parts,), jnp.float32, low / len(cuts), top_value / len(cuts))
        gain = gain * jnp.repeat(jnp.exp(heights), shape[axis_at] // parts).reshape((-1,) + (1,) * (len(shape) - 1 - axis_at))
    return gain


def gaussian(rng, dims, spread, bound, cuts=(), kind=jnp.bfloat16):
    values = jax.random.normal(rng, dims, jnp.float32) * spread
    if len(cuts) > 0:
        values = block_levels(rng, dims, cuts, -0.22, 0.18) * values
    return jnp.clip(values, min=-bound, max=bound).astype(kind)


def setup_inputs(seed: int = 0) -> dict:
    key_list = jax.random.split(jax.random.key(seed), 5)
    return {
        "green": gaussian(key_list[0], (RECEIVER_COUNT, CELLS), CELLS ** -0.5, 0.03125, ((0, 2), (1, 16)), jnp.float32),
        "field": gaussian(key_list[1], (CELLS, SOURCE_COUNT), 1.0, 6.0, ((0, 16),), jnp.float32),
        "probe": gaussian(key_list[2], (PROBE_COUNT, CELLS), 1.0, 6.0, ((1, 16),), jnp.float32),
        "cov_inv": draw_cov_inv(jax.random.fold_in(key_list[4], 71), 0),
    }


def reference(green, field, probe, cov_inv):
    highest_precision = lax.Precision.HIGHEST
    sensitivity_blocks = CELLS // CELL_DEV
    g_blocks = green.reshape(RECEIVER_COUNT, sensitivity_blocks, CELL_DEV).transpose(1, 0, 2)
    f_blocks = field.reshape(sensitivity_blocks, CELL_DEV, SOURCE_COUNT)
    p_blocks = probe.reshape(PROBE_COUNT, sensitivity_blocks, CELL_DEV).transpose(1, 0, 2)

    def forward(total, pieces):
        g_part, f_part, p_part = pieces
        lifted = (f_part[:, :, None] * p_part.T[:, None, :]).reshape(CELL_DEV, SOURCE_COUNT * PROBE_COUNT)
        return total + jnp.dot(g_part, lifted, precision=highest_precision, preferred_element_type=jnp.float32), None

    measured_data, _ = lax.scan(forward, jnp.zeros((RECEIVER_COUNT, SOURCE_COUNT * PROBE_COUNT), jnp.float32), (g_blocks, f_blocks, p_blocks))
    whitened_data = jnp.dot(cov_inv, measured_data, precision=highest_precision, preferred_element_type=jnp.float32)
    curvature = jnp.einsum("dou,dob->ub", measured_data.reshape(RECEIVER_COUNT, SOURCE_COUNT, PROBE_COUNT), whitened_data.reshape(RECEIVER_COUNT, SOURCE_COUNT, PROBE_COUNT), precision=highest_precision) / (RECEIVER_COUNT * SOURCE_COUNT)

    def backward(pieces):
        g_part, f_part = pieces
        back = jnp.dot(g_part.T, whitened_data, precision=highest_precision, preferred_element_type=jnp.float32).reshape(CELL_DEV, SOURCE_COUNT, PROBE_COUNT)
        return jnp.einsum("cs,csp->pc", f_part, back, precision=highest_precision)

    hess = lax.map(backward, (g_blocks, f_blocks))
    hessian = hess.transpose(1, 0, 2).reshape(PROBE_COUNT, CELLS)
    return hessian, curvature
```

```python
import functools

import jax
import jax.numpy as jnp
from jax import lax
from jax.experimental import pallas as pl
from jax.experimental.pallas import tpu as pltpu
from jax.sharding import PartitionSpec as P


F32 = jnp.float32
BF16 = jnp.bfloat16
FACTOR = 1
ROWS = 8


def split(x):
    high = x.astype(BF16)
    return high, (x - high.astype(F32)).astype(BF16)


def dot_nn(a, b):
    return jnp.dot(a, b, preferred_element_type=F32)


def dot_nt(a, b):
    return lax.dot_general(a, b, (((1,), (1,)), ((), ())), preferred_element_type=F32)


def stage_groups(devices):
    bits = devices.bit_length() - 1
    groups = [[0]] if bits > 0 else []
    rest = list(range(1, bits))
    if len(rest) % 2:
        groups.append([rest.pop(0)])
    while rest:
        groups.append([rest.pop(0), rest.pop(0)])
    return [[m << g[0] for m in range(2 ** len(g))][::-1] for g in groups]


def row_order(groups):
    order = [0]
    for masks in groups[::-1]:
        order = [m | o for m in masks for o in order]
    return order


def forward_kernel(order, blk, tile, make_g, me_ref, f_ref, p_ref, *refs):
    refs = list(refs)
    g_refs = [refs.pop(0)] if make_g else [refs.pop(0), refs.pop(0)]
    send_ref, keep_ref, ft_ref = refs.pop(0), refs.pop(0), refs.pop(0)
    if make_g:
        gh_ref, gl_ref = refs.pop(0), refs.pop(0)
    else:
        gh_ref, gl_ref = g_refs
    lh_ref, ll_ref = refs
    me = me_ref[0]
    cells = p_ref.shape[1]
    probes = p_ref.shape[0]
    half = send_ref.shape[0]
    for c in range(0, cells, tile):
        cols = slice(c, c + tile)
        ft_ref[:, cols] = f_ref[cols, :].T
        if make_g:
            gh, gl = split(g_refs[0][:, cols])
            gh_ref[:, cols] = gh
            gl_ref[:, cols] = gl
        else:
            gh, gl = gh_ref[:, cols], gl_ref[:, cols]
        at = 0
        for rel in order:
            base = ft_ref[pl.ds(pl.multiple_of((me ^ rel) * blk, blk), blk), cols]
            rows = jnp.concatenate([base * p_ref[p : p + 1, cols] for p in range(probes)], axis=0)
            high, low = split(rows)
            lh_ref[at : at + rows.shape[0], cols] = high
            ll_ref[at : at + rows.shape[0], cols] = low
            at += rows.shape[0]
        for out_ref, lo in ((send_ref, 0), (keep_ref, half)):
            lh, ll = lh_ref[lo : lo + half, cols], ll_ref[lo : lo + half, cols]
            part = dot_nt(lh, gh) + dot_nt(lh, gl) + dot_nt(ll, gh)
            if c == 0:
                out_ref[...] = part
            else:
                out_ref[...] += part


VMEM = pl.BlockSpec(memory_space=pltpu.VMEM)
SMEM = pl.BlockSpec(memory_space=pltpu.SMEM)


def call(kernel, name, flops, out_shape, *args, scratch=(), scalars=1, limit=32 << 20):
    shapes = jax.tree.leaves(out_shape)
    size = sum(x.size * x.dtype.itemsize for x in list(args) + shapes)
    return pl.pallas_call(
        kernel,
        out_shape=out_shape,
        in_specs=[SMEM] * scalars + [VMEM] * (len(args) - scalars),
        out_specs=jax.tree.map(lambda _: VMEM, out_shape),
        scratch_shapes=list(scratch),
        compiler_params=pltpu.CompilerParams(vmem_limit_bytes=limit),
        cost_estimate=pl.CostEstimate(flops=flops, bytes_accessed=size, transcendentals=0),
        name=name,
    )(*args)


def forward(me, source, probe, green, order, make_g):
    receivers, cells = green[0].shape
    n = source.shape[1]
    total = n * probe.shape[0]
    out_shape = [jax.ShapeDtypeStruct((total // 2, receivers), F32)] * 2
    out_shape.append(jax.ShapeDtypeStruct((n, cells), F32))
    if make_g:
        out_shape += [jax.ShapeDtypeStruct((receivers, cells), BF16)] * 2
    return call(
        functools.partial(forward_kernel, order, n // len(order), min(512, cells), make_g),
        "forward", 6 * total * receivers * cells, out_shape,
        me, source, probe, *green,
        scratch=[pltpu.VMEM((total, cells), BF16)] * 2,
    )


def white_kernel(rcv_ref, mine_ref, other_ref, ch_ref, cl_ref, out_ref):
    half = mine_ref.shape[1]
    m = mine_ref.shape[0]
    rcv = rcv_ref[0]
    total = None
    for ref, at in ((mine_ref, rcv), (other_ref, 1 - rcv)):
        cols = pl.ds(pl.multiple_of(at * half, half), half)
        high, low = split(ref[...])
        both = jnp.concatenate([high, low], axis=0)
        ch = ch_ref[:, cols]
        first = dot_nt(both, ch)
        part = first[:m] + first[m:] + dot_nt(high, cl_ref[:, cols])
        total = part if total is None else total + part
    out_ref[...] = total


def whiten(rcv, mine, other, ch, cl):
    return call(
        white_kernel, "whiten", 6 * mine.shape[0] * ch.shape[0] * ch.shape[1],
        jax.ShapeDtypeStruct((mine.shape[0], ch.shape[0]), F32),
        rcv, mine, other, ch, cl,
    )


def split_kernel(c_ref, ch_ref, cl_ref):
    ch_ref[...], cl_ref[...] = split(c_ref[...])


def split_of(c):
    return call(split_kernel, "split", c.size, [jax.ShapeDtypeStruct(c.shape, BF16)] * 2, c, scalars=0)


def backward_kernel(order, blk, tile, pieces, first, last, me_ref, *refs):
    w_refs, refs = refs[:pieces], list(refs[pieces:])
    gh_ref, gl_ref, ft_ref = refs.pop(0), refs.pop(0), refs.pop(0)
    in_ref = None if first else refs.pop(0)
    out_ref, wh_ref, wl_ref, back_ref = refs
    me = me_ref[0]
    cells = gh_ref.shape[1]
    at = 0
    for w_ref in w_refs:
        high, low = split(w_ref[...])
        wh_ref[at : at + w_ref.shape[0], :] = high
        wl_ref[at : at + w_ref.shape[0], :] = low
        at += w_ref.shape[0]
    wh, wl = wh_ref[...], wl_ref[...]
    probes = wh.shape[0] // (blk * len(order))
    for c in range(0, cells, tile):
        cols = slice(c, c + tile)
        gh, gl = gh_ref[:, cols], gl_ref[:, cols]
        back_ref[...] = dot_nn(wh, gh) + dot_nn(wh, gl) + dot_nn(wl, gh)
        sums = [
            jnp.zeros((ROWS, tile), F32) if first else in_ref[p * ROWS : (p + 1) * ROWS, cols]
            for p in range(probes)
        ]
        at = 0
        for rel in order:
            base = ft_ref[pl.ds(pl.multiple_of((me ^ rel) * blk, blk), blk), cols]
            for p in range(probes):
                for r in range(0, blk, ROWS):
                    sums[p] = sums[p] + base[r : r + ROWS] * back_ref[at : at + ROWS, :]
                    at += ROWS
        for p in range(probes):
            if last:
                out_ref[p : p + 1, cols] = jnp.sum(sums[p], axis=0, keepdims=True)
            else:
                out_ref[p * ROWS : (p + 1) * ROWS, cols] = sums[p]


def backward(me, white, gh, gl, ft, so_far, order, probes, last):
    receivers, cells = gh.shape
    n = ft.shape[0]
    total = n * probes
    tile = min(512, cells)
    first = so_far is None
    return call(
        functools.partial(backward_kernel, order, n // len(order), tile, len(white), first, last),
        "backward", 6 * total * receivers * cells,
        jax.ShapeDtypeStruct((probes * (1 if last else ROWS), cells), F32),
        me, *white, gh, gl, ft, *([] if first else [so_far]),
        scratch=[pltpu.VMEM((total, receivers), BF16)] * 2 + [pltpu.VMEM((total, tile), F32)],
    )


def gram_kernel(blk, count, *refs):
    d_refs, w_refs, out_ref = refs[:count], refs[count : 2 * count], refs[2 * count]
    total = None
    for d_ref, w_ref in zip(d_refs, w_refs):
        part = lax.dot_general(
            d_ref[...], w_ref[...], (((1,), (1,)), ((), ())),
            precision=lax.Precision.HIGHEST, preferred_element_type=F32,
        )
        total = part if total is None else total + part
    size = total.shape[0]
    row = lax.broadcasted_iota(jnp.int32, total.shape, 0)
    col = lax.broadcasted_iota(jnp.int32, total.shape, 1)
    total = jnp.where(row % blk == col % blk, total, 0.0)
    across = lax.broadcasted_iota(jnp.int32, (size, out_ref.shape[1]), 0) // blk
    pick = jnp.where(across == lax.broadcasted_iota(jnp.int32, across.shape, 1), 1.0, 0.0)
    wide = jnp.dot(total, pick, precision=lax.Precision.HIGHEST, preferred_element_type=F32)
    out_ref[...] = jnp.zeros_like(out_ref)
    for p in range(size // blk):
        out_ref[p : p + 1, :] = jnp.sum(wide[p * blk : (p + 1) * blk], axis=0, keepdims=True)


def gram_of(data, white, blk):
    return call(
        functools.partial(gram_kernel, blk, len(data)), "gram", 1,
        jax.ShapeDtypeStruct((ROWS, 128), F32), *data, *white, scalars=0,
    )


def exchange(x, axis, size, mask):
    return lax.ppermute(x, axis, [(i, i ^ mask) for i in range(size)])


def local(cell_size, rcv_size, green, field, probe, cov_inv):
    sources = field.shape[1]
    probes = probe.shape[0]
    receivers = cov_inv.shape[1]
    groups = stage_groups(cell_size)
    order = row_order(groups)
    n = max(ROWS * cell_size, 128) * FACTOR
    chunks = sources // n
    blk = n // cell_size
    me = lax.axis_index("cell").reshape(1).astype(jnp.int32)
    rcv = lax.axis_index("rcv").reshape(1).astype(jnp.int32)
    ch, cl = split_of(cov_inv)
    gh = gl = None
    transposed, mine, white, gathered = [], [], [], []
    halves = []
    for k in range(chunks):
        out = forward(me, field[:, k * n : (k + 1) * n], probe, [green] if k == 0 else [gh, gl], order, k == 0)
        halves.append(out[:2])
        transposed.append(out[2])
        if k == 0:
            gh, gl = out[3:]
    for k in range(chunks):
        send, keep = halves[k]
        rows = keep + exchange(send, "cell", cell_size, groups[0][0])
        for masks in groups[1:]:
            size = rows.shape[0] // len(masks)
            parts = [rows[i * size : (i + 1) * size] for i in range(len(masks))]
            rows = parts[-1]
            for part, mask in zip(parts[:-1], masks[:-1]):
                rows = rows + exchange(part, "cell", cell_size, mask)
        mine.append(rows)
        other = exchange(rows, "rcv", rcv_size, 1)
        white.append(whiten(rcv, rows, other, ch, cl))
    for k in range(chunks):
        rows = white[k]
        for masks in groups[:1:-1]:
            rows = jnp.concatenate([exchange(rows, "cell", cell_size, m) for m in masks[:-1]] + [rows], axis=0)
        quarters = [rows]
        for masks in groups[1::-1]:
            quarters = [exchange(q, "cell", cell_size, m) for m in masks[:-1] for q in quarters] + quarters
        gathered.append(quarters)
    hess = None
    for k in range(chunks):
        hess = backward(me, gathered[k], gh, gl, transposed[k], hess, order, probes, k == chunks - 1)
    hessian = hess + exchange(hess, "rcv", rcv_size, 1)

    gram = gram_of(mine, white, blk)
    for masks in groups:
        gram = sum([exchange(gram, "cell", cell_size, m) for m in masks[:-1]], gram)
    gram = gram + exchange(gram, "rcv", rcv_size, 1)
    curvature = gram[:probes, :probes] / (receivers * sources)
    return (hessian, curvature)


def solution(mesh):
    return jax.shard_map(
        functools.partial(local, mesh.shape["cell"], mesh.shape["rcv"]),
        mesh=mesh,
        in_specs=(P("rcv", "cell"), P("cell", None), P(None, "cell"), P("rcv", None)),
        out_specs=(P(None, "cell"), P()),
        check_vma=False,
    )
```

```python
import functools

import jax
import jax.numpy as jnp
from jax import lax
from jax.experimental import pallas as pl
from jax.experimental.pallas import tpu as pltpu
from jax.sharding import PartitionSpec as P


F32 = jnp.float32
BF16 = jnp.bfloat16
SHARE = ((1,), (1,), (1,), (1,))
ROWS = 8
LANES = 128


def split(x):
    high = x.astype(BF16)
    return high, (x - high.astype(F32)).astype(BF16)


def dot_nn(a, b):
    return jnp.dot(a, b, preferred_element_type=F32)


def dot_nt(a, b):
    return lax.dot_general(a, b, (((1,), (1,)), ((), ())), preferred_element_type=F32)


def stage_groups(devices):
    masks = [1 << bit for bit in range(devices.bit_length() - 1)]
    return [[m, 0] for m in masks[:-1]], masks[-1]


def row_order(groups):
    order = [0]
    for masks in groups[::-1]:
        order = [m | o for m in masks for o in order]
    return order


def forward_kernel(order, blk, tile, lane, make_g, me_ref, *refs):
    refs = list(refs)
    p_ref, f_ref = refs.pop(0), refs.pop(0)
    g_refs = [refs.pop(0)] if make_g else [refs.pop(0), refs.pop(0)]
    send_ref, keep_ref, ft_ref = refs.pop(0), refs.pop(0), refs.pop(0)
    if make_g:
        gh_ref, gl_ref = refs.pop(0), refs.pop(0)
    else:
        gh_ref, gl_ref = g_refs
    lh_ref, ll_ref = refs.pop(0), refs.pop(0)
    me = me_ref[0]
    cells = p_ref.shape[1]
    probes = p_ref.shape[0]
    half = send_ref.shape[0]
    n = ft_ref.shape[0]
    copies = []
    if make_g:
        f_buf, g_buf, p_buf, f_sem, g_sem, p_sem = refs
        p_copy = pltpu.make_async_copy(p_ref, p_buf, p_sem)
        p_copy.start()
        for t, c in enumerate(range(0, cells, tile)):
            cols = pl.ds(c, tile)
            copies.append(
                (
                    pltpu.make_async_copy(f_ref.at[cols, pl.ds(lane, n)], f_buf.at[cols, :], f_sem.at[t]),
                    pltpu.make_async_copy(g_refs[0].at[:, cols], g_buf.at[:, cols], g_sem.at[t]),
                )
            )
        for pair in copies:
            for copy in pair:
                copy.start()
        p_ref = p_buf
    for t, c in enumerate(range(0, cells, tile)):
        cols = slice(c, c + tile)
        if make_g:
            for copy in copies[t] + ((p_copy,) if t == 0 else ()):
                copy.wait()
            ft_ref[:, cols] = f_buf[cols, :].T
            gh, gl = split(g_buf[:, cols])
            gh_ref[:, cols] = gh
            gl_ref[:, cols] = gl
        else:
            ft_ref[:, cols] = f_ref[cols, lane : lane + n].T
            gh, gl = gh_ref[:, cols], gl_ref[:, cols]
        at = 0
        for rel in order:
            base = ft_ref[pl.ds(pl.multiple_of((me ^ rel) * blk, blk), blk), cols]
            rows = jnp.concatenate([base * p_ref[p : p + 1, cols] for p in range(probes)], axis=0)
            high, low = split(rows)
            lh_ref[at : at + rows.shape[0], cols] = high
            ll_ref[at : at + rows.shape[0], cols] = low
            at += rows.shape[0]
        for out_ref, lo in ((send_ref, 0), (keep_ref, half)):
            lh, ll = lh_ref[lo : lo + half, cols], ll_ref[lo : lo + half, cols]
            part = dot_nt(lh, gh) + dot_nt(lh, gl) + dot_nt(ll, gh)
            if c == 0:
                out_ref[...] = part
            else:
                out_ref[...] += part


VMEM = pl.BlockSpec(memory_space=pltpu.VMEM)
SMEM = pl.BlockSpec(memory_space=pltpu.SMEM)


def call(kernel, flops, out_shape, *args, scratch=(), scalars=1, raw=0):
    shapes = jax.tree.leaves(out_shape)
    held = [x for x in scratch if getattr(x, "memory_space", None) == pltpu.VMEM]
    limit = sum(x.inner_aval.size * x.inner_aval.dtype.itemsize for x in held) * 5 // 4 + (4 << 20)
    size = sum(x.size * x.dtype.itemsize for x in list(args) + shapes)
    vmem = len(args) - scalars - raw
    cut = len(args) - raw
    args = list(args[:cut]) + [pltpu.with_memory_space_constraint(x, pltpu.HBM) for x in args[cut:]]
    return pl.pallas_call(
        kernel,
        out_shape=out_shape,
        in_specs=[SMEM] * scalars + [VMEM] * vmem + [pl.BlockSpec(memory_space=pltpu.HBM)] * raw,
        out_specs=jax.tree.map(lambda _: VMEM, out_shape),
        scratch_shapes=list(scratch),
        compiler_params=pltpu.CompilerParams(vmem_limit_bytes=min(limit, 60 << 20)),
        cost_estimate=pl.CostEstimate(flops=flops, bytes_accessed=size, transcendentals=0),
    )(*args)


def rows_of(count, like):
    return jax.ShapeDtypeStruct((count, like.shape[1]), F32)


def forward(me, source, probe, green, k, n, order, make_g):
    receivers, cells = green[0].shape
    total = n * probe.shape[0]
    tile = min(512, cells)
    out_shape = [jax.ShapeDtypeStruct((total // 2, receivers), F32)] * 2
    out_shape.append(jax.ShapeDtypeStruct((n, cells), F32))
    scratch = [pltpu.VMEM((total, cells), BF16)] * 2
    if make_g:
        out_shape += [jax.ShapeDtypeStruct((receivers, cells), BF16)] * 2
        scratch += [pltpu.VMEM((cells, n), F32), pltpu.VMEM((receivers, cells), F32), pltpu.VMEM(probe.shape, F32)]
        scratch += [pltpu.SemaphoreType.DMA((cells // tile,))] * 2 + [pltpu.SemaphoreType.DMA]
    return call(
        functools.partial(forward_kernel, order, n // len(order), tile, k * n, make_g),
        6 * total * receivers * cells, out_shape,
        me, probe, source, *green, scratch=scratch, raw=3 if make_g else 0,
    )


def core_add_kernel(keep_ref, got_ref, send_ref, stay_ref):
    half = send_ref.shape[0]
    send_ref[...] = keep_ref[:half] + got_ref[:half]
    stay_ref[...] = keep_ref[half:] + got_ref[half:]


def core_add(keep, got):
    return call(core_add_kernel, keep.size, [rows_of(keep.shape[0] // 2, keep)] * 2, keep, got, scalars=0)


def total_kernel(*refs):
    total = refs[0][...]
    for ref in refs[1:-1]:
        total = total + ref[...]
    refs[-1][...] = total


def total_of(parts):
    return call(total_kernel, parts[0].size, rows_of(parts[0].shape[0], parts[0]), *parts, scalars=0)


def merge_kernel(count, rows, *refs):
    ins, outs = refs[: 2 * count], refs[2 * count :]
    blocks = ins[0].shape[0] // rows
    inner = blocks // len(outs)
    for i in range(blocks):
        for k in range(count):
            at = ((i % inner) * count + k) * rows
            outs[i // inner][at : at + rows] = (
                ins[2 * k][i * rows : (i + 1) * rows] + ins[2 * k + 1][i * rows : (i + 1) * rows]
            )


def merge(pairs, pieces, rows):
    flat = [x for pair in pairs for x in pair]
    size = flat[0].shape[0] * len(pairs) // pieces
    return call(
        functools.partial(merge_kernel, len(pairs), rows), flat[0].size,
        [rows_of(size, flat[0])] * pieces, *flat, scalars=0,
    )


def collect_kernel(count, rows, extra, *refs):
    outs = refs[len(refs) - count :]
    ins = refs[: len(refs) - count]
    inner = (ins[0].shape[0] - extra) // (rows * count)
    for i in range(len(ins) * inner):
        for k in range(count):
            at = ((i % inner) * count + k) * rows
            outs[k][i * rows : (i + 1) * rows] = ins[i // inner][at : at + rows]
    if extra:
        total = ins[0][ins[0].shape[0] - extra :]
        for ref in ins[1:]:
            total = total + ref[ref.shape[0] - extra :]
        outs[-1][outs[-1].shape[0] - extra :] = total


def collect(pieces, count, rows, extra):
    size = (pieces[0].shape[0] - extra) * len(pieces) // count
    shapes = [rows_of(size, pieces[0])] * (count - 1) + [rows_of(size + extra, pieces[0])]
    return call(functools.partial(collect_kernel, count, rows, extra), 1, shapes, *pieces, scalars=0)


def white_kernel(blk, probes, first, count, rcv_ref, *refs):
    refs = list(refs)
    mine_refs, there_refs = refs[:count], refs[count : 2 * count]
    ch_ref, cl_ref = refs[2 * count : 2 * count + 2]
    refs = refs[2 * count + 2 :]
    so_far = None if first else refs.pop(0)
    out_ref = refs[0]
    half = mine_refs[0].shape[1]
    m = sum(ref.shape[0] for ref in mine_refs)
    rcv = rcv_ref[0]
    mine = jnp.concatenate([ref[...] for ref in mine_refs], axis=0)
    there = jnp.concatenate([ref[...] for ref in there_refs], axis=0)
    total = None
    for x, at in ((mine, rcv), (there, 1 - rcv)):
        cols = pl.ds(pl.multiple_of(at * half, half), half)
        high, low = split(x)
        both = jnp.concatenate([high, low], axis=0)
        product = dot_nt(both, ch_ref[:, cols])
        part = product[:m] + product[m:] + dot_nt(high, cl_ref[:, cols])
        total = part if total is None else total + part
    out_ref[:m] = total
    lines = []
    for p in range(probes):
        for q in range(probes):
            line = None
            for g in range(0, m, blk * probes):
                for r in range(0, blk, ROWS):
                    at, to = g + p * blk + r, g + q * blk + r
                    part = mine[at : at + ROWS] * total[to : to + ROWS]
                    line = part if line is None else line + part
            lines.append(jnp.sum(line, axis=0, keepdims=True))
    gram = jnp.concatenate(lines, axis=0)
    if so_far is not None:
        gram = gram + so_far[...]
    if len(refs) > 1:
        refs[1][...] = gram
    else:
        out_ref[m:] = gram


def whiten(rcv, mine, there, ch, cl, blk, probes, so_far, joined):
    first = so_far is None
    m = sum(x.shape[0] for x in mine)
    sizes = [m + probes**2] if joined else [m, probes**2]
    return call(
        functools.partial(white_kernel, blk, probes, first, len(mine)),
        6 * m * ch.shape[0] * ch.shape[1], [rows_of(size, mine[0]) for size in sizes],
        rcv, *mine, *there, ch, cl, *([] if first else [so_far]),
    )


def split_kernel(c_ref, ch_ref, cl_ref):
    ch_ref[...], cl_ref[...] = split(c_ref[...])


def split_of(c):
    return call(split_kernel, c.size, [jax.ShapeDtypeStruct(c.shape, BF16)] * 2, c, scalars=0)


def backward_kernel(order, blk, tile, pieces, first, last, me_ref, *refs):
    w_refs, refs = refs[:pieces], list(refs[pieces:])
    gh_ref, gl_ref, ft_ref = refs.pop(0), refs.pop(0), refs.pop(0)
    in_ref = None if first else refs.pop(0)
    out_ref, wh_ref, wl_ref, back_ref = refs
    me = me_ref[0]
    cells = gh_ref.shape[1]
    quarter = wh_ref.shape[0] // pieces
    for i, w_ref in enumerate(w_refs):
        high, low = split(w_ref[:quarter])
        wh_ref[i * quarter : (i + 1) * quarter, :] = high
        wl_ref[i * quarter : (i + 1) * quarter, :] = low
    wh, wl = wh_ref[...], wl_ref[...]
    probes = wh.shape[0] // (blk * len(order))
    for c in range(0, cells, tile):
        cols = slice(c, c + tile)
        gh, gl = gh_ref[:, cols], gl_ref[:, cols]
        back_ref[...] = dot_nn(wh, gh) + dot_nn(wh, gl) + dot_nn(wl, gh)
        sums = [
            jnp.zeros((ROWS, tile), F32) if first else in_ref[p * ROWS : (p + 1) * ROWS, cols]
            for p in range(probes)
        ]
        at = 0
        for rel in order:
            base = ft_ref[pl.ds(pl.multiple_of((me ^ rel) * blk, blk), blk), cols]
            for p in range(probes):
                for r in range(0, blk, ROWS):
                    sums[p] = sums[p] + base[r : r + ROWS] * back_ref[at : at + ROWS, :]
                    at += ROWS
        for p in range(probes):
            if last:
                out_ref[p : p + 1, cols] = jnp.sum(sums[p], axis=0, keepdims=True)
            else:
                out_ref[p * ROWS : (p + 1) * ROWS, cols] = sums[p]
    if last and w_refs[0].shape[0] > quarter:
        gram = w_refs[0][quarter:]
        for w_ref in w_refs[1:]:
            gram = gram + w_ref[quarter:]
        sums = jnp.sum(gram, axis=1, keepdims=True)
        for i in range(probes**2):
            at = cells + i % probes * LANES
            out_ref[i // probes : i // probes + 1, at : at + LANES] = jnp.broadcast_to(sums[i : i + 1], (1, LANES))
    elif last:
        out_ref[:, cells:] = jnp.zeros((probes, probes * LANES), F32)


def backward(me, white, gh, gl, ft, so_far, order, probes, last):
    receivers, cells = gh.shape
    n = ft.shape[0]
    total = n * probes
    tile = min(512, cells)
    first = so_far is None
    return call(
        functools.partial(backward_kernel, order, n // len(order), tile, len(white), first, last),
        6 * total * receivers * cells,
        jax.ShapeDtypeStruct((probes, cells + probes * LANES) if last else (probes * ROWS, cells), F32),
        me, *white, gh, gl, ft, *([] if first else [so_far]),
        scratch=[pltpu.VMEM((total, receivers), BF16)] * 2 + [pltpu.VMEM((total, tile), F32)],
    )


def final_kernel(scale, mine_ref, there_ref, hessian_ref, curvature_ref):
    probes, cells = hessian_ref.shape
    hessian_ref[...] = mine_ref[:, :cells] + there_ref[:, :cells]
    for q in range(probes):
        lane = cells + q * LANES
        curvature_ref[:, q : q + 1] = (mine_ref[:, lane : lane + 1] + there_ref[:, lane : lane + 1]) / scale


def final(mine, there, cells, scale):
    probes = mine.shape[0]
    return call(
        functools.partial(final_kernel, scale), mine.size,
        [jax.ShapeDtypeStruct((probes, size), F32) for size in (cells, probes)], mine, there, scalars=0,
    )


def local(cell_size, rcv_size, green, field, probe, cov_inv):
    sources = field.shape[1]
    probes = probe.shape[0]
    receivers = cov_inv.shape[1]
    groups, far_mask = stage_groups(cell_size)
    order = row_order(groups)
    n = max(ROWS * len(order), 128)
    chunks = sources // n
    blk = n // len(order)
    rows = blk * probes
    share = SHARE if sum(map(sum, SHARE)) == chunks else ((chunks,),)
    extra = probes**2 if len(groups) == 3 else 0
    me = (lax.axis_index("cell") % far_mask).reshape(1).astype(jnp.int32)
    rcv = lax.axis_index("rcv").reshape(1).astype(jnp.int32)

    def swap(x, mask):
        return lax.ppermute(x, "cell", [(i, i ^ mask) for i in range(cell_size)])

    def across(x):
        return lax.ppermute(x, "rcv", [(i, i ^ 1) for i in range(rcv_size)])

    core_mask, near_mask = groups[0][0], groups[1][0]
    ch, cl = split_of(cov_inv)
    gh = gl = gram = hess = None
    transposed, reduced = [], []
    for k in range(chunks):
        out = forward(me, field, probe, [green] if k == 0 else [gh, gl], k, n, order, k == 0)
        if k == 0:
            gh, gl = out[3:]
        transposed.append(out[2])
        send, stay = core_add(out[1], swap(out[0], core_mask))
        reduced.append((stay, swap(send, near_mask)))
    gathered = [None] * chunks
    j = k = 0
    for i, counts in enumerate(share):
        mine, there, pair = [], [], []
        for count in counts:
            now = range(k, k + count)
            pair += now
            k += count
            pieces = merge([reduced[c] for c in now], len(groups[2]), rows)
            for g, masks in enumerate(groups[2:]):
                if g:
                    size = own.shape[0] // len(masks)
                    pieces = [own[c * size : (c + 1) * size] for c in range(len(masks))]
                got = [swap(x, m) for x, m in zip(pieces[:-1], masks[:-1])]
                own = total_of(got + [pieces[-1]])
            own = total_of([swap(own, far_mask), own])
            mine.append(own)
            there.append(across(own))
            j += 1
        joined = extra > 0 and i == len(share) - 1
        white = whiten(rcv, mine, there, ch, cl, blk, probes, gram, joined)
        gram = white[-1]
        own = white[0]
        for g, masks in list(enumerate(groups[2:]))[::-1]:
            pieces = [swap(own, m) for m in masks[:-1]] + [own]
            if g:
                own = jnp.concatenate(pieces, axis=0)
        parts = collect(pieces, len(pair), rows, extra if joined else 0)
        for c, part in zip(pair, parts):
            got = swap(part, near_mask)
            near = swap(part, core_mask)
            gathered[c] = [swap(got, core_mask), near, got, part]
    for k in range(chunks):
        hess = backward(me, gathered[k], gh, gl, transposed[k], hess, order, probes, k == chunks - 1)
    hessian, curvature = final(hess, across(hess), field.shape[0], receivers * sources)
    if not extra:
        curvature = lax.psum(jnp.sum(gram, axis=1).reshape(probes, probes), ("cell", "rcv")) / (receivers * sources)
    return (hessian, curvature)


def solution(mesh):
    def body(*args):
        return local(mesh.shape["cell"], mesh.shape["rcv"], *args)

    return jax.shard_map(
        body,
        mesh=mesh,
        in_specs=(P("rcv", "cell"), P("cell", None), P(None, "cell"), P("rcv", None)),
        out_specs=(P(None, "cell"), P()),
        check_vma=False,
    )
```

```python
import functools

import jax
import jax.numpy as jnp
from jax import lax
from jax.experimental import pallas as pl
from jax.experimental.pallas import tpu as pltpu
from jax.sharding import PartitionSpec as P


F32 = jnp.float32
BF16 = jnp.bfloat16
SHARE = ((1,), (1,), (1,), (1,))
ROWS = 8
LANES = 128


def split(x):
    high = x.astype(BF16)
    return high, (x - high.astype(F32)).astype(BF16)


def dot_nn(a, b):
    return jnp.dot(a, b, preferred_element_type=F32)


def dot_nt(a, b):
    return lax.dot_general(a, b, (((1,), (1,)), ((), ())), preferred_element_type=F32)


def stage_groups(devices):
    masks = [1 << bit for bit in range(devices.bit_length() - 1)]
    return [[m, 0] for m in masks[:-1]], masks[-1]


def row_order(groups):
    order = [0]
    for masks in groups[::-1]:
        order = [m | o for m in masks for o in order]
    return order


def forward_kernel(order, blk, tile, lane, make_g, me_ref, *refs):
    refs = list(refs)
    p_ref, f_ref = refs.pop(0), refs.pop(0)
    g_refs = [refs.pop(0)] if make_g else [refs.pop(0), refs.pop(0)]
    send_ref, keep_ref, ft_ref = refs.pop(0), refs.pop(0), refs.pop(0)
    if make_g:
        gh_ref, gl_ref = refs.pop(0), refs.pop(0)
    else:
        gh_ref, gl_ref = g_refs
    lh_ref, ll_ref = refs.pop(0), refs.pop(0)
    me = me_ref[0]
    cells = p_ref.shape[1]
    probes = p_ref.shape[0]
    half = send_ref.shape[0]
    n = ft_ref.shape[0]
    copies = []
    if make_g:
        f_buf, g_buf, p_buf, f_sem, g_sem, p_sem = refs
        p_copy = pltpu.make_async_copy(p_ref, p_buf, p_sem)
        p_copy.start()
        for t, c in enumerate(range(0, cells, tile)):
            cols = pl.ds(c, tile)
            copies.append(
                (
                    pltpu.make_async_copy(f_ref.at[cols, pl.ds(lane, n)], f_buf.at[cols, :], f_sem.at[t]),
                    pltpu.make_async_copy(g_refs[0].at[:, cols], g_buf.at[:, cols], g_sem.at[t]),
                )
            )
        for pair in copies[:2]:
            for copy in pair:
                copy.start()
        p_ref = p_buf
    for t, c in enumerate(range(0, cells, tile)):
        cols = slice(c, c + tile)
        if make_g:
            for copy in copies[t] + ((p_copy,) if t == 0 else ()):
                copy.wait()
            for pair in copies[t + 2 : t + 3]:
                for copy in pair:
                    copy.start()
            ft_ref[:, cols] = f_buf[cols, :].T
            gh, gl = split(g_buf[:, cols])
            gh_ref[:, cols] = gh
            gl_ref[:, cols] = gl
        else:
            ft_ref[:, cols] = f_ref[cols, lane : lane + n].T
            gh, gl = gh_ref[:, cols], gl_ref[:, cols]
        at = 0
        for rel in order:
            base = ft_ref[pl.ds(pl.multiple_of((me ^ rel) * blk, blk), blk), cols]
            rows = jnp.concatenate([base * p_ref[p : p + 1, cols] for p in range(probes)], axis=0)
            high, low = split(rows)
            lh_ref[at : at + rows.shape[0], cols] = high
            ll_ref[at : at + rows.shape[0], cols] = low
            at += rows.shape[0]
        for out_ref, lo in ((send_ref, 0), (keep_ref, half)):
            lh, ll = lh_ref[lo : lo + half, cols], ll_ref[lo : lo + half, cols]
            part = dot_nt(lh, gh) + dot_nt(lh, gl) + dot_nt(ll, gh)
            if c == 0:
                out_ref[...] = part
            else:
                out_ref[...] += part


VMEM = pl.BlockSpec(memory_space=pltpu.VMEM)
SMEM = pl.BlockSpec(memory_space=pltpu.SMEM)


def call(kernel, flops, out_shape, *args, scratch=(), scalars=1, raw=0):
    shapes = jax.tree.leaves(out_shape)
    held = [x for x in scratch if getattr(x, "memory_space", None) == pltpu.VMEM]
    limit = sum(x.inner_aval.size * x.inner_aval.dtype.itemsize for x in held) * 5 // 4 + (4 << 20)
    size = sum(x.size * x.dtype.itemsize for x in list(args) + shapes)
    vmem = len(args) - scalars - raw
    cut = len(args) - raw
    args = list(args[:cut]) + [pltpu.with_memory_space_constraint(x, pltpu.HBM) for x in args[cut:]]
    return pl.pallas_call(
        kernel,
        out_shape=out_shape,
        in_specs=[SMEM] * scalars + [VMEM] * vmem + [pl.BlockSpec(memory_space=pltpu.HBM)] * raw,
        out_specs=jax.tree.map(lambda _: VMEM, out_shape),
        scratch_shapes=list(scratch),
        compiler_params=pltpu.CompilerParams(vmem_limit_bytes=min(limit, 60 << 20)),
        cost_estimate=pl.CostEstimate(flops=flops, bytes_accessed=size, transcendentals=0),
    )(*args)


def rows_of(count, like):
    return jax.ShapeDtypeStruct((count, like.shape[1]), F32)


def forward(me, source, probe, green, k, n, order, make_g):
    receivers, cells = green[0].shape
    total = n * probe.shape[0]
    tile = min(512, cells)
    out_shape = [jax.ShapeDtypeStruct((total // 2, receivers), F32)] * 2
    out_shape.append(jax.ShapeDtypeStruct((n, cells), F32))
    scratch = [pltpu.VMEM((total, cells), BF16)] * 2
    if make_g:
        out_shape += [jax.ShapeDtypeStruct((receivers, cells), BF16)] * 2
        scratch += [pltpu.VMEM((cells, n), F32), pltpu.VMEM((receivers, cells), F32), pltpu.VMEM(probe.shape, F32)]
        scratch += [pltpu.SemaphoreType.DMA((cells // tile,))] * 2 + [pltpu.SemaphoreType.DMA]
    return call(
        functools.partial(forward_kernel, order, n // len(order), tile, k * n, make_g),
        6 * total * receivers * cells, out_shape,
        me, probe, source, *green, scratch=scratch, raw=3 if make_g else 0,
    )


def core_add_kernel(keep_ref, got_ref, send_ref, stay_ref):
    half = send_ref.shape[0]
    send_ref[...] = keep_ref[:half] + got_ref[:half]
    stay_ref[...] = keep_ref[half:] + got_ref[half:]


def core_add(keep, got):
    return call(core_add_kernel, keep.size, [rows_of(keep.shape[0] // 2, keep)] * 2, keep, got, scalars=0)


def total_kernel(*refs):
    total = refs[0][...]
    for ref in refs[1:-1]:
        total = total + ref[...]
    refs[-1][...] = total


def total_of(parts):
    return call(total_kernel, parts[0].size, rows_of(parts[0].shape[0], parts[0]), *parts, scalars=0)


def merge_kernel(count, rows, *refs):
    ins, outs = refs[: 2 * count], refs[2 * count :]
    blocks = ins[0].shape[0] // rows
    inner = blocks // len(outs)
    for i in range(blocks):
        for k in range(count):
            at = ((i % inner) * count + k) * rows
            outs[i // inner][at : at + rows] = (
                ins[2 * k][i * rows : (i + 1) * rows] + ins[2 * k + 1][i * rows : (i + 1) * rows]
            )


def merge(pairs, pieces, rows):
    flat = [x for pair in pairs for x in pair]
    size = flat[0].shape[0] * len(pairs) // pieces
    return call(
        functools.partial(merge_kernel, len(pairs), rows), flat[0].size,
        [rows_of(size, flat[0])] * pieces, *flat, scalars=0,
    )


def collect_kernel(count, rows, extra, *refs):
    outs = refs[len(refs) - count :]
    ins = refs[: len(refs) - count]
    inner = (ins[0].shape[0] - extra) // (rows * count)
    for i in range(len(ins) * inner):
        for k in range(count):
            at = ((i % inner) * count + k) * rows
            outs[k][i * rows : (i + 1) * rows] = ins[i // inner][at : at + rows]
    if extra:
        total = ins[0][ins[0].shape[0] - extra :]
        for ref in ins[1:]:
            total = total + ref[ref.shape[0] - extra :]
        outs[-1][outs[-1].shape[0] - extra :] = total


def collect(pieces, count, rows, extra):
    size = (pieces[0].shape[0] - extra) * len(pieces) // count
    shapes = [rows_of(size, pieces[0])] * (count - 1) + [rows_of(size + extra, pieces[0])]
    return call(functools.partial(collect_kernel, count, rows, extra), 1, shapes, *pieces, scalars=0)


def white_kernel(blk, probes, first, count, rcv_ref, *refs):
    refs = list(refs)
    mine_refs, there_refs = refs[:count], refs[count : 2 * count]
    ch_ref, cl_ref = refs[2 * count : 2 * count + 2]
    refs = refs[2 * count + 2 :]
    so_far = None if first else refs.pop(0)
    out_ref = refs[0]
    half = mine_refs[0].shape[1]
    m = sum(ref.shape[0] for ref in mine_refs)
    rcv = rcv_ref[0]
    mine = jnp.concatenate([ref[...] for ref in mine_refs], axis=0)
    there = jnp.concatenate([ref[...] for ref in there_refs], axis=0)
    total = None
    for x, at in ((mine, rcv), (there, 1 - rcv)):
        cols = pl.ds(pl.multiple_of(at * half, half), half)
        high, low = split(x)
        both = jnp.concatenate([high, low], axis=0)
        product = dot_nt(both, ch_ref[:, cols])
        part = product[:m] + product[m:] + dot_nt(high, cl_ref[:, cols])
        total = part if total is None else total + part
    out_ref[:m] = total
    lines = []
    for p in range(probes):
        for q in range(probes):
            line = None
            for g in range(0, m, blk * probes):
                for r in range(0, blk, ROWS):
                    at, to = g + p * blk + r, g + q * blk + r
                    part = mine[at : at + ROWS] * total[to : to + ROWS]
                    line = part if line is None else line + part
            lines.append(jnp.sum(line, axis=0, keepdims=True))
    gram = jnp.concatenate(lines, axis=0)
    if so_far is not None:
        gram = gram + so_far[...]
    if len(refs) > 1:
        refs[1][...] = gram
    else:
        out_ref[m:] = gram


def whiten(rcv, mine, there, ch, cl, blk, probes, so_far, joined):
    first = so_far is None
    m = sum(x.shape[0] for x in mine)
    sizes = [m + probes**2] if joined else [m, probes**2]
    return call(
        functools.partial(white_kernel, blk, probes, first, len(mine)),
        6 * m * ch.shape[0] * ch.shape[1], [rows_of(size, mine[0]) for size in sizes],
        rcv, *mine, *there, ch, cl, *([] if first else [so_far]),
    )


def split_kernel(c_ref, ch_ref, cl_ref):
    ch_ref[...], cl_ref[...] = split(c_ref[...])


def split_of(c):
    return call(split_kernel, c.size, [jax.ShapeDtypeStruct(c.shape, BF16)] * 2, c, scalars=0)


def backward_kernel(order, blk, tile, pieces, first, last, me_ref, *refs):
    w_refs, refs = refs[:pieces], list(refs[pieces:])
    gh_ref, gl_ref, ft_ref = refs.pop(0), refs.pop(0), refs.pop(0)
    in_ref = None if first else refs.pop(0)
    out_ref, wh_ref, wl_ref, back_ref = refs
    me = me_ref[0]
    cells = gh_ref.shape[1]
    quarter = wh_ref.shape[0] // pieces
    for i, w_ref in enumerate(w_refs):
        high, low = split(w_ref[:quarter])
        wh_ref[i * quarter : (i + 1) * quarter, :] = high
        wl_ref[i * quarter : (i + 1) * quarter, :] = low
    wh, wl = wh_ref[...], wl_ref[...]
    probes = wh.shape[0] // (blk * len(order))
    for c in range(0, cells, tile):
        cols = slice(c, c + tile)
        gh, gl = gh_ref[:, cols], gl_ref[:, cols]
        back_ref[...] = dot_nn(wh, gh) + dot_nn(wh, gl) + dot_nn(wl, gh)
        sums = [
            jnp.zeros((ROWS, tile), F32) if first else in_ref[p * ROWS : (p + 1) * ROWS, cols]
            for p in range(probes)
        ]
        at = 0
        for rel in order:
            base = ft_ref[pl.ds(pl.multiple_of((me ^ rel) * blk, blk), blk), cols]
            for p in range(probes):
                for r in range(0, blk, ROWS):
                    sums[p] = sums[p] + base[r : r + ROWS] * back_ref[at : at + ROWS, :]
                    at += ROWS
        for p in range(probes):
            if last:
                out_ref[p : p + 1, cols] = jnp.sum(sums[p], axis=0, keepdims=True)
            else:
                out_ref[p * ROWS : (p + 1) * ROWS, cols] = sums[p]
    if last and w_refs[0].shape[0] > quarter:
        gram = w_refs[0][quarter:]
        for w_ref in w_refs[1:]:
            gram = gram + w_ref[quarter:]
        sums = jnp.sum(gram, axis=1, keepdims=True)
        for i in range(probes**2):
            at = cells + i % probes * LANES
            out_ref[i // probes : i // probes + 1, at : at + LANES] = jnp.broadcast_to(sums[i : i + 1], (1, LANES))
    elif last:
        out_ref[:, cells:] = jnp.zeros((probes, probes * LANES), F32)


def backward(me, white, gh, gl, ft, so_far, order, probes, last):
    receivers, cells = gh.shape
    n = ft.shape[0]
    total = n * probes
    tile = min(512, cells)
    first = so_far is None
    return call(
        functools.partial(backward_kernel, order, n // len(order), tile, len(white), first, last),
        6 * total * receivers * cells,
        jax.ShapeDtypeStruct((probes, cells + probes * LANES) if last else (probes * ROWS, cells), F32),
        me, *white, gh, gl, ft, *([] if first else [so_far]),
        scratch=[pltpu.VMEM((total, receivers), BF16)] * 2 + [pltpu.VMEM((total, tile), F32)],
    )


def final_kernel(scale, mine_ref, there_ref, hessian_ref, curvature_ref):
    probes, cells = hessian_ref.shape
    hessian_ref[...] = mine_ref[:, :cells] + there_ref[:, :cells]
    for q in range(probes):
        lane = cells + q * LANES
        curvature_ref[:, q : q + 1] = (mine_ref[:, lane : lane + 1] + there_ref[:, lane : lane + 1]) / scale


def final(mine, there, cells, scale):
    probes = mine.shape[0]
    return call(
        functools.partial(final_kernel, scale), mine.size,
        [jax.ShapeDtypeStruct((probes, size), F32) for size in (cells, probes)], mine, there, scalars=0,
    )


def local(cell_size, rcv_size, green, field, probe, cov_inv):
    sources = field.shape[1]
    probes = probe.shape[0]
    receivers = cov_inv.shape[1]
    groups, far_mask = stage_groups(cell_size)
    order = row_order(groups)
    n = max(ROWS * len(order), 128)
    chunks = sources // n
    blk = n // len(order)
    rows = blk * probes
    share = SHARE if sum(map(sum, SHARE)) == chunks else ((chunks,),)
    extra = probes**2 if len(groups) == 3 else 0
    me = (lax.axis_index("cell") % far_mask).reshape(1).astype(jnp.int32)
    rcv = lax.axis_index("rcv").reshape(1).astype(jnp.int32)

    def swap(x, mask):
        return lax.ppermute(x, "cell", [(i, i ^ mask) for i in range(cell_size)])

    def across(x):
        return lax.ppermute(x, "rcv", [(i, i ^ 1) for i in range(rcv_size)])

    core_mask, near_mask = groups[0][0], groups[1][0]
    ch, cl = split_of(cov_inv)
    gh = gl = gram = hess = None
    transposed, reduced = [], []
    for k in range(chunks):
        out = forward(me, field, probe, [green] if k == 0 else [gh, gl], k, n, order, k == 0)
        if k == 0:
            gh, gl = out[3:]
        transposed.append(out[2])
        send, stay = core_add(out[1], swap(out[0], core_mask))
        reduced.append((stay, swap(send, near_mask)))
    gathered = [None] * chunks
    j = k = 0
    for i, counts in enumerate(share):
        mine, there, pair = [], [], []
        for count in counts:
            now = range(k, k + count)
            pair += now
            k += count
            pieces = merge([reduced[c] for c in now], len(groups[2]), rows)
            for g, masks in enumerate(groups[2:]):
                if g:
                    size = own.shape[0] // len(masks)
                    pieces = [own[c * size : (c + 1) * size] for c in range(len(masks))]
                got = [swap(x, m) for x, m in zip(pieces[:-1], masks[:-1])]
                own = total_of(got + [pieces[-1]])
            own = total_of([swap(own, far_mask), own])
            mine.append(own)
            there.append(across(own))
            j += 1
        joined = extra > 0 and i == len(share) - 1
        white = whiten(rcv, mine, there, ch, cl, blk, probes, gram, joined)
        gram = white[-1]
        own = white[0]
        for g, masks in list(enumerate(groups[2:]))[::-1]:
            pieces = [swap(own, m) for m in masks[:-1]] + [own]
            if g:
                own = jnp.concatenate(pieces, axis=0)
        parts = collect(pieces, len(pair), rows, extra if joined else 0)
        for c, part in zip(pair, parts):
            got = swap(part, near_mask)
            near = swap(part, core_mask)
            gathered[c] = [swap(got, core_mask), near, got, part]
    for k in range(chunks):
        hess = backward(me, gathered[k], gh, gl, transposed[k], hess, order, probes, k == chunks - 1)
    hessian, curvature = final(hess, across(hess), field.shape[0], receivers * sources)
    if not extra:
        curvature = lax.psum(jnp.sum(gram, axis=1).reshape(probes, probes), ("cell", "rcv")) / (receivers * sources)
    return (hessian, curvature)


def solution(mesh):
    def body(*args):
        return local(mesh.shape["cell"], mesh.shape["rcv"], *args)

    return jax.shard_map(
        body,
        mesh=mesh,
        in_specs=(P("rcv", "cell"), P("cell", None), P(None, "cell"), P("rcv", None)),
        out_specs=(P(None, "cell"), P()),
        check_vma=False,
    )
```

```python
import functools

import jax
import jax.numpy as jnp
from jax import lax
from jax.experimental import pallas as pl
from jax.experimental.pallas import tpu as pltpu
from jax.sharding import PartitionSpec as P


F32 = jnp.float32
BF16 = jnp.bfloat16
SHARE = ((1,), (1,), (1,), (1,))
ROWS = 8
LANES = 128


def split(x):
    high = x.astype(BF16)
    return high, (x - high.astype(F32)).astype(BF16)


def dot_nn(a, b):
    return jnp.dot(a, b, preferred_element_type=F32)


def dot_nt(a, b):
    return lax.dot_general(a, b, (((1,), (1,)), ((), ())), preferred_element_type=F32)


def stage_groups(devices):
    masks = [1 << bit for bit in range(devices.bit_length() - 1)]
    return [[m, 0] for m in masks[:-1]], masks[-1]


def row_order(groups):
    order = [0]
    for masks in groups[::-1]:
        order = [m | o for m in masks for o in order]
    return order


def forward_kernel(order, blk, tile, lane, make_g, me_ref, *refs):
    refs = list(refs)
    p_ref, f_ref = refs.pop(0), refs.pop(0)
    g_refs = [refs.pop(0)] if make_g else [refs.pop(0), refs.pop(0)]
    send_ref, keep_ref, ft_ref = refs.pop(0), refs.pop(0), refs.pop(0)
    if make_g:
        gh_ref, gl_ref = refs.pop(0), refs.pop(0)
    else:
        gh_ref, gl_ref = g_refs
    lh_ref, ll_ref = refs.pop(0), refs.pop(0)
    me = me_ref[0]
    cells = p_ref.shape[1]
    probes = p_ref.shape[0]
    half = send_ref.shape[0]
    n = ft_ref.shape[0]
    copies = []
    if make_g:
        f_buf, g_buf, p_buf, f_sem, g_sem, p_sem = refs
        p_copy = pltpu.make_async_copy(p_ref, p_buf, p_sem)
        p_copy.start()
        for t, c in enumerate(range(0, cells, tile)):
            cols = pl.ds(c, tile)
            copies.append(
                (
                    pltpu.make_async_copy(f_ref.at[cols, pl.ds(lane, n)], f_buf.at[cols, :], f_sem.at[t]),
                    pltpu.make_async_copy(g_refs[0].at[:, cols], g_buf.at[:, cols], g_sem.at[t]),
                )
            )
        for pair in copies[:4]:
            for copy in pair:
                copy.start()
        p_ref = p_buf
    for t, c in enumerate(range(0, cells, tile)):
        cols = slice(c, c + tile)
        if make_g:
            for copy in copies[t] + ((p_copy,) if t == 0 else ()):
                copy.wait()
            for pair in copies[t + 4 : t + 5]:
                for copy in pair:
                    copy.start()
            ft_ref[:, cols] = f_buf[cols, :].T
            gh, gl = split(g_buf[:, cols])
            gh_ref[:, cols] = gh
            gl_ref[:, cols] = gl
        else:
            ft_ref[:, cols] = f_ref[cols, lane : lane + n].T
            gh, gl = gh_ref[:, cols], gl_ref[:, cols]
        at = 0
        for rel in order:
            base = ft_ref[pl.ds(pl.multiple_of((me ^ rel) * blk, blk), blk), cols]
            rows = jnp.concatenate([base * p_ref[p : p + 1, cols] for p in range(probes)], axis=0)
            high, low = split(rows)
            lh_ref[at : at + rows.shape[0], cols] = high
            ll_ref[at : at + rows.shape[0], cols] = low
            at += rows.shape[0]
        for out_ref, lo in ((send_ref, 0), (keep_ref, half)):
            lh, ll = lh_ref[lo : lo + half, cols], ll_ref[lo : lo + half, cols]
            part = dot_nt(lh, gh) + dot_nt(lh, gl) + dot_nt(ll, gh)
            if c == 0:
                out_ref[...] = part
            else:
                out_ref[...] += part


VMEM = pl.BlockSpec(memory_space=pltpu.VMEM)
SMEM = pl.BlockSpec(memory_space=pltpu.SMEM)


def call(kernel, flops, out_shape, *args, scratch=(), scalars=1, raw=0):
    shapes = jax.tree.leaves(out_shape)
    held = [x for x in scratch if getattr(x, "memory_space", None) == pltpu.VMEM]
    limit = sum(x.inner_aval.size * x.inner_aval.dtype.itemsize for x in held) * 5 // 4 + (4 << 20)
    size = sum(x.size * x.dtype.itemsize for x in list(args) + shapes)
    vmem = len(args) - scalars - raw
    cut = len(args) - raw
    args = list(args[:cut]) + [pltpu.with_memory_space_constraint(x, pltpu.HBM) for x in args[cut:]]
    return pl.pallas_call(
        kernel,
        out_shape=out_shape,
        in_specs=[SMEM] * scalars + [VMEM] * vmem + [pl.BlockSpec(memory_space=pltpu.HBM)] * raw,
        out_specs=jax.tree.map(lambda _: VMEM, out_shape),
        scratch_shapes=list(scratch),
        compiler_params=pltpu.CompilerParams(vmem_limit_bytes=min(limit, 60 << 20)),
        cost_estimate=pl.CostEstimate(flops=flops, bytes_accessed=size, transcendentals=0),
    )(*args)


def rows_of(count, like):
    return jax.ShapeDtypeStruct((count, like.shape[1]), F32)


def forward(me, source, probe, green, k, n, order, make_g):
    receivers, cells = green[0].shape
    total = n * probe.shape[0]
    tile = min(256 if make_g else 512, cells)
    out_shape = [jax.ShapeDtypeStruct((total // 2, receivers), F32)] * 2
    out_shape.append(jax.ShapeDtypeStruct((n, cells), F32))
    scratch = [pltpu.VMEM((total, cells), BF16)] * 2
    if make_g:
        out_shape += [jax.ShapeDtypeStruct((receivers, cells), BF16)] * 2
        scratch += [pltpu.VMEM((cells, n), F32), pltpu.VMEM((receivers, cells), F32), pltpu.VMEM(probe.shape, F32)]
        scratch += [pltpu.SemaphoreType.DMA((cells // tile,))] * 2 + [pltpu.SemaphoreType.DMA]
    return call(
        functools.partial(forward_kernel, order, n // len(order), tile, k * n, make_g),
        6 * total * receivers * cells, out_shape,
        me, probe, source, *green, scratch=scratch, raw=3 if make_g else 0,
    )


def core_add_kernel(keep_ref, got_ref, send_ref, stay_ref):
    half = send_ref.shape[0]
    send_ref[...] = keep_ref[:half] + got_ref[:half]
    stay_ref[...] = keep_ref[half:] + got_ref[half:]


def core_add(keep, got):
    return call(core_add_kernel, keep.size, [rows_of(keep.shape[0] // 2, keep)] * 2, keep, got, scalars=0)


def total_kernel(*refs):
    total = refs[0][...]
    for ref in refs[1:-1]:
        total = total + ref[...]
    refs[-1][...] = total


def total_of(parts):
    return call(total_kernel, parts[0].size, rows_of(parts[0].shape[0], parts[0]), *parts, scalars=0)


def merge_kernel(count, rows, *refs):
    ins, outs = refs[: 2 * count], refs[2 * count :]
    blocks = ins[0].shape[0] // rows
    inner = blocks // len(outs)
    for i in range(blocks):
        for k in range(count):
            at = ((i % inner) * count + k) * rows
            outs[i // inner][at : at + rows] = (
                ins[2 * k][i * rows : (i + 1) * rows] + ins[2 * k + 1][i * rows : (i + 1) * rows]
            )


def merge(pairs, pieces, rows):
    flat = [x for pair in pairs for x in pair]
    size = flat[0].shape[0] * len(pairs) // pieces
    return call(
        functools.partial(merge_kernel, len(pairs), rows), flat[0].size,
        [rows_of(size, flat[0])] * pieces, *flat, scalars=0,
    )


def collect_kernel(count, rows, extra, *refs):
    outs = refs[len(refs) - count :]
    ins = refs[: len(refs) - count]
    inner = (ins[0].shape[0] - extra) // (rows * count)
    for i in range(len(ins) * inner):
        for k in range(count):
            at = ((i % inner) * count + k) * rows
            outs[k][i * rows : (i + 1) * rows] = ins[i // inner][at : at + rows]
    if extra:
        total = ins[0][ins[0].shape[0] - extra :]
        for ref in ins[1:]:
            total = total + ref[ref.shape[0] - extra :]
        outs[-1][outs[-1].shape[0] - extra :] = total


def collect(pieces, count, rows, extra):
    size = (pieces[0].shape[0] - extra) * len(pieces) // count
    shapes = [rows_of(size, pieces[0])] * (count - 1) + [rows_of(size + extra, pieces[0])]
    return call(functools.partial(collect_kernel, count, rows, extra), 1, shapes, *pieces, scalars=0)


def white_kernel(blk, probes, first, count, rcv_ref, *refs):
    refs = list(refs)
    mine_refs, there_refs = refs[:count], refs[count : 2 * count]
    ch_ref, cl_ref = refs[2 * count : 2 * count + 2]
    refs = refs[2 * count + 2 :]
    so_far = None if first else refs.pop(0)
    out_ref = refs[0]
    half = mine_refs[0].shape[1]
    m = sum(ref.shape[0] for ref in mine_refs)
    rcv = rcv_ref[0]
    mine = jnp.concatenate([ref[...] for ref in mine_refs], axis=0)
    there = jnp.concatenate([ref[...] for ref in there_refs], axis=0)
    total = None
    for x, at in ((mine, rcv), (there, 1 - rcv)):
        cols = pl.ds(pl.multiple_of(at * half, half), half)
        high, low = split(x)
        both = jnp.concatenate([high, low], axis=0)
        product = dot_nt(both, ch_ref[:, cols])
        part = product[:m] + product[m:] + dot_nt(high, cl_ref[:, cols])
        total = part if total is None else total + part
    out_ref[:m] = total
    lines = []
    for p in range(probes):
        for q in range(probes):
            line = None
            for g in range(0, m, blk * probes):
                for r in range(0, blk, ROWS):
                    at, to = g + p * blk + r, g + q * blk + r
                    part = mine[at : at + ROWS] * total[to : to + ROWS]
                    line = part if line is None else line + part
            lines.append(jnp.sum(line, axis=0, keepdims=True))
    gram = jnp.concatenate(lines, axis=0)
    if so_far is not None:
        gram = gram + so_far[...]
    if len(refs) > 1:
        refs[1][...] = gram
    else:
        out_ref[m:] = gram


def whiten(rcv, mine, there, ch, cl, blk, probes, so_far, joined):
    first = so_far is None
    m = sum(x.shape[0] for x in mine)
    sizes = [m + probes**2] if joined else [m, probes**2]
    return call(
        functools.partial(white_kernel, blk, probes, first, len(mine)),
        6 * m * ch.shape[0] * ch.shape[1], [rows_of(size, mine[0]) for size in sizes],
        rcv, *mine, *there, ch, cl, *([] if first else [so_far]),
    )


def split_kernel(c_ref, ch_ref, cl_ref):
    ch_ref[...], cl_ref[...] = split(c_ref[...])


def split_of(c):
    return call(split_kernel, c.size, [jax.ShapeDtypeStruct(c.shape, BF16)] * 2, c, scalars=0)


def backward_kernel(order, blk, tile, pieces, first, last, me_ref, *refs):
    w_refs, refs = refs[:pieces], list(refs[pieces:])
    gh_ref, gl_ref, ft_ref = refs.pop(0), refs.pop(0), refs.pop(0)
    in_ref = None if first else refs.pop(0)
    out_ref, wh_ref, wl_ref, back_ref = refs
    me = me_ref[0]
    cells = gh_ref.shape[1]
    quarter = wh_ref.shape[0] // pieces
    for i, w_ref in enumerate(w_refs):
        high, low = split(w_ref[:quarter])
        wh_ref[i * quarter : (i + 1) * quarter, :] = high
        wl_ref[i * quarter : (i + 1) * quarter, :] = low
    wh, wl = wh_ref[...], wl_ref[...]
    probes = wh.shape[0] // (blk * len(order))
    for c in range(0, cells, tile):
        cols = slice(c, c + tile)
        gh, gl = gh_ref[:, cols], gl_ref[:, cols]
        back_ref[...] = dot_nn(wh, gh) + dot_nn(wh, gl) + dot_nn(wl, gh)
        sums = [
            jnp.zeros((ROWS, tile), F32) if first else in_ref[p * ROWS : (p + 1) * ROWS, cols]
            for p in range(probes)
        ]
        at = 0
        for rel in order:
            base = ft_ref[pl.ds(pl.multiple_of((me ^ rel) * blk, blk), blk), cols]
            for p in range(probes):
                for r in range(0, blk, ROWS):
                    sums[p] = sums[p] + base[r : r + ROWS] * back_ref[at : at + ROWS, :]
                    at += ROWS
        for p in range(probes):
            if last:
                out_ref[p : p + 1, cols] = jnp.sum(sums[p], axis=0, keepdims=True)
            else:
                out_ref[p * ROWS : (p + 1) * ROWS, cols] = sums[p]
    if last and w_refs[0].shape[0] > quarter:
        gram = w_refs[0][quarter:]
        for w_ref in w_refs[1:]:
            gram = gram + w_ref[quarter:]
        sums = jnp.sum(gram, axis=1, keepdims=True)
        for i in range(probes**2):
            at = cells + i % probes * LANES
            out_ref[i // probes : i // probes + 1, at : at + LANES] = jnp.broadcast_to(sums[i : i + 1], (1, LANES))
    elif last:
        out_ref[:, cells:] = jnp.zeros((probes, probes * LANES), F32)


def backward(me, white, gh, gl, ft, so_far, order, probes, last):
    receivers, cells = gh.shape
    n = ft.shape[0]
    total = n * probes
    tile = min(512, cells)
    first = so_far is None
    return call(
        functools.partial(backward_kernel, order, n // len(order), tile, len(white), first, last),
        6 * total * receivers * cells,
        jax.ShapeDtypeStruct((probes, cells + probes * LANES) if last else (probes * ROWS, cells), F32),
        me, *white, gh, gl, ft, *([] if first else [so_far]),
        scratch=[pltpu.VMEM((total, receivers), BF16)] * 2 + [pltpu.VMEM((total, tile), F32)],
    )


def final_kernel(scale, mine_ref, there_ref, hessian_ref, curvature_ref):
    probes, cells = hessian_ref.shape
    hessian_ref[...] = mine_ref[:, :cells] + there_ref[:, :cells]
    for q in range(probes):
        lane = cells + q * LANES
        curvature_ref[:, q : q + 1] = (mine_ref[:, lane : lane + 1] + there_ref[:, lane : lane + 1]) / scale


def final(mine, there, cells, scale):
    probes = mine.shape[0]
    return call(
        functools.partial(final_kernel, scale), mine.size,
        [jax.ShapeDtypeStruct((probes, size), F32) for size in (cells, probes)], mine, there, scalars=0,
    )


def local(cell_size, rcv_size, green, field, probe, cov_inv):
    sources = field.shape[1]
    probes = probe.shape[0]
    receivers = cov_inv.shape[1]
    groups, far_mask = stage_groups(cell_size)
    order = row_order(groups)
    n = max(ROWS * len(order), 128)
    chunks = sources // n
    blk = n // len(order)
    rows = blk * probes
    share = SHARE if sum(map(sum, SHARE)) == chunks else ((chunks,),)
    extra = probes**2 if len(groups) == 3 else 0
    me = (lax.axis_index("cell") % far_mask).reshape(1).astype(jnp.int32)
    rcv = lax.axis_index("rcv").reshape(1).astype(jnp.int32)

    def swap(x, mask):
        return lax.ppermute(x, "cell", [(i, i ^ mask) for i in range(cell_size)])

    def across(x):
        return lax.ppermute(x, "rcv", [(i, i ^ 1) for i in range(rcv_size)])

    core_mask, near_mask = groups[0][0], groups[1][0]
    ch, cl = split_of(cov_inv)
    gh = gl = gram = hess = None
    transposed, reduced = [], []
    for k in range(chunks):
        out = forward(me, field, probe, [green] if k == 0 else [gh, gl], k, n, order, k == 0)
        if k == 0:
            gh, gl = out[3:]
        transposed.append(out[2])
        send, stay = core_add(out[1], swap(out[0], core_mask))
        reduced.append((stay, swap(send, near_mask)))
    gathered = [None] * chunks
    j = k = 0
    for i, counts in enumerate(share):
        mine, there, pair = [], [], []
        for count in counts:
            now = range(k, k + count)
            pair += now
            k += count
            pieces = merge([reduced[c] for c in now], len(groups[2]), rows)
            for g, masks in enumerate(groups[2:]):
                if g:
                    size = own.shape[0] // len(masks)
                    pieces = [own[c * size : (c + 1) * size] for c in range(len(masks))]
                got = [swap(x, m) for x, m in zip(pieces[:-1], masks[:-1])]
                own = total_of(got + [pieces[-1]])
            own = total_of([swap(own, far_mask), own])
            mine.append(own)
            there.append(across(own))
            j += 1
        joined = extra > 0 and i == len(share) - 1
        white = whiten(rcv, mine, there, ch, cl, blk, probes, gram, joined)
        gram = white[-1]
        own = white[0]
        for g, masks in list(enumerate(groups[2:]))[::-1]:
            pieces = [swap(own, m) for m in masks[:-1]] + [own]
            if g:
                own = jnp.concatenate(pieces, axis=0)
        parts = collect(pieces, len(pair), rows, extra if joined else 0)
        for c, part in zip(pair, parts):
            got = swap(part, near_mask)
            near = swap(part, core_mask)
            gathered[c] = [swap(got, core_mask), near, got, part]
    for k in range(chunks):
        hess = backward(me, gathered[k], gh, gl, transposed[k], hess, order, probes, k == chunks - 1)
    hessian, curvature = final(hess, across(hess), field.shape[0], receivers * sources)
    if not extra:
        curvature = lax.psum(jnp.sum(gram, axis=1).reshape(probes, probes), ("cell", "rcv")) / (receivers * sources)
    return (hessian, curvature)


def solution(mesh):
    def body(*args):
        return local(mesh.shape["cell"], mesh.shape["rcv"], *args)

    return jax.shard_map(
        body,
        mesh=mesh,
        in_specs=(P("rcv", "cell"), P("cell", None), P(None, "cell"), P("rcv", None)),
        out_specs=(P(None, "cell"), P()),
        check_vma=False,
    )
```
